32 devices in a mesh: seg: 8 (over z, x), grp: 4 (over y, core).
Axes of the slice: x: 2, y: 2, z: 4, core: 2. Of those that a mesh axis runs over, the one named last changes fastest.
Arguments:
- initial_state: float32 [512], replicated, may hold values from -6 to 6
- transition: float32 [512, 512], replicated, as said below
- gains: float32 [512], replicated, may hold values from 0 to 1, as said below
- tiles: float32 [4, 4096, 512], P('grp', 'seg'), may hold values from -16 to 16
- tile_owner: int32 [4, 4096, 1], P('grp', 'seg'), may hold values from 0 to 31; in each aligned block of 512 rows (0 to 511, 512 to 1023, ..., all dimensions but the last counted through in order) at most 40 rows name the same one
- tile_step: int32 [4, 4096], P('grp', 'seg'), may hold values from 0 to 31
Outputs:
- states: float32 [4, 256, 512], P('grp', 'seg')
The draws below stay inside these ranges and needn't reach their ends.
Inputs may be any that keep to these rules, and one draw needn't show every extreme that they name: `tile_owner`: among the tiles of one device no owner is named more than 40 times, and in some devices one owner is named exactly 40 times. `transition`: diagonal entries lie strictly between 0 and 1. `gains`: every gain is positive.
All inputs are finite; a program needn't handle non-finite values.
Results may differ from the reference program's by a relative error of at most 0.0003.
Values sent between devices are 32-bit elements; how exact they have to be, the bound alone decides.
A program may use at most 192 MiB of HBM per device.

```python
import math
import jax
import jax.numpy as jnp
import numpy as np
from jax import lax

W = 512
STEP_DEV = 32
TILE_DEV = 512
CAP = 40
STEPS = 1024
TILES = 16384
N_SEG = 8
N_GRP = 4


def mode_pick(key):
    return jax.random.randint(jax.random.fold_in(key, 11), (W,), 0, 8)


def log_between(key, lower, upper):
    unit = jax.random.uniform(key, (W,), jnp.float32)
    return jnp.exp(math.log(lower) + unit * (math.log(upper) - math.log(lower)))


def signed_hadamard(key):
    row_ids = jnp.arange(W, dtype=jnp.int32)
    column_order = jax.random.permutation(jax.random.fold_in(key, 1), W).astype(jnp.int32)
    common_bits = jnp.bitwise_and(row_ids[:, None], column_order[None, :])
    parity = jnp.zeros((W, W), jnp.int32)
    for bit_place in range(W.bit_length()):
        parity = parity + jnp.bitwise_and(jnp.right_shift(common_bits, bit_place), 1)
    row_signs = 2 * jax.random.randint(jax.random.fold_in(key, 2), (W,), 0, 2) - 1
    column_signs = 2 * jax.random.randint(jax.random.fold_in(key, 3), (W,), 0, 2) - 1
    sign_table = (1 - 2 * (parity % 2)) * row_signs[:, None] * column_signs[None, :]
    return sign_table.astype(jnp.float32) * (1.0 / math.sqrt(W))


def draw_transition(key, part):
    slow = mode_pick(key) < 4
    first_share = 0.5
    slow_rate = log_between(jax.random.fold_in(key, 21), 0.1 / STEPS, 0.5 / STEPS)
    fast_rate = log_between(jax.random.fold_in(key, 22), 0.01, 0.03)
    diagonal = jnp.exp(-jnp.where(slow, slow_rate, fast_rate))
    mixing = 4.0 / max(STEPS, 1024)
    first_table = signed_hadamard(jax.random.fold_in(key, 23))
    second_table = signed_hadamard(jax.random.fold_in(key, 24))
    rotation = first_share * (first_table - first_table.T) + (1.0 - first_share) * (second_table - second_table.T)
    identity = jnp.eye(W, dtype=jnp.float32)
    blended = identity + mixing * rotation
    return diagonal[:, None] * blended


def draw_gains(key, part):
    slow = mode_pick(key) < 4
    per_step = STEP_DEV / TILE_DEV
    slow_gain = log_between(jax.random.fold_in(key, 31), 0.1 / TILES, 0.4 / TILES)
    fast_gain = log_between(jax.random.fold_in(key, 32), 0.01 * per_step, 0.1 * per_step)
    return jnp.where(slow, slow_gain, fast_gain)


def set_ends(result, stream_key, least, high):
    shape = result.shape
    spot = [jax.random.randint(jax.random.fold_in(stream_key, axis), (), 0, shape[axis]) for axis in range(len(shape))]
    result = result.at[tuple(spot)].set(least)
    longest = shape.index(max(shape))
    spot[longest] = (spot[longest] + 1) % shape[longest]
    return result.at[tuple(spot)].set(high)


def block_scale(own_key, extent, shards, least, high):
    level = 1.0
    for axis_at, shards_of in shards:
        steps = jax.random.uniform(jax.random.fold_in(jax.random.fold_in(own_key, 6), axis_at), (shards_of,), jnp.float32, least / len(shards), high / len(shards))
        level = level * jnp.repeat(jnp.exp(steps), extent[axis_at] // shards_of).reshape((-1,) + (1,) * (len(extent) - 1 - axis_at))
    return level


def rank_bounds(amount, lean):
    loads = [(1 << 20) // math.isqrt(standing ** lean) + 1 for standing in range(1, amount + 1)]
    scale = 1 + sum(loads) // (1 << 30)
    return np.cumsum(np.array([max(1, weight // scale) for weight in loads]))


def ranked_ids(rng, shape, count, lean):
    table = rank_bounds(count, lean)
    lot = jax.random.randint(jax.random.fold_in(rng, 1), shape, 0, int(table[count - 1]))
    rank = jnp.searchsorted(jnp.asarray(table, jnp.int32), lot, side="right")
    return jax.random.permutation(jax.random.fold_in(rng, 2), count)[rank].astype(jnp.int32)


def routed_block(stream_key, own, number, rows, amount, top, bound, slope):
    order = jax.random.permutation(stream_key, amount)
    crowded, ordinary = portions_of(amount, rows * top, bound, slope, True), portions_of(amount, rows * top, bound, slope, False)
    places = jnp.arange(amount)

    def named(sizes, offset_by):
        used = int((sizes > 0).sum())
        fixed = max(1, used // 4)
        shifted = fixed + (places - fixed + offset_by * (used - fixed)) % max(1, amount - fixed)
        return jnp.zeros((amount,), jnp.int32).at[order[jnp.where(places < fixed, places, shifted)]].set(jnp.asarray(sizes, jnp.int32))

    sizes = jnp.where(number % 4 == 0, named(crowded, number // 4), named(ordinary, number - number // 4 - 1))
    mixed = jax.random.permutation(jax.random.fold_in(own, 3), amount)
    source_of, receiver = mixed[0:amount // 2 * 2:2], mixed[1:amount // 2 * 2:2]
    room = jnp.minimum(sizes[source_of] - 1, bound - sizes[receiver]) // 2
    room = jnp.where((source_of == order[0]) | (receiver == order[0]) | (sizes[receiver] == 0), 0, jnp.maximum(room, 0))
    shifted = jax.random.randint(jax.random.fold_in(own, 4), (amount // 2,), 0, 1 << 20) % (room + 1)
    sizes = sizes.at[source_of].add(-shifted).at[receiver].add(shifted)
    members = jnp.searchsorted(jnp.cumsum(sizes), jnp.arange(rows * top), side="right").astype(jnp.int32)
    table = members.reshape(top, rows).T
    table = table[jax.random.permutation(jax.random.fold_in(own, 1), rows)]
    offset_by = jax.random.randint(jax.random.fold_in(own, 2), (rows, 1), 0, top)
    return jnp.take_along_axis(table, (jnp.arange(top)[None, :] + offset_by) % top, axis=1)


def portions_of(count, total, most, lean, full):
    portions = [(1 << 20) // math.isqrt(grade ** lean) + 1 for grade in range(1, count + 1)]
    largest = most if full else min(most, max(-(-total // count), total * portions[0] // sum(portions)))
    least = 1 if total - largest >= count - 1 else 0
    holding, rest = [largest] + [least] * (count - 1), total - largest - least * (count - 1)
    while rest > 0:
        candidates = [i for i in range(1, count) if holding[i] < largest] or [i for i in range(1, count) if holding[i] < most]
        mass, remaining = sum([portions[i] for i in candidates]), rest
        for i in candidates:
            addition = min(most - holding[i], max(1, remaining * portions[i] // mass), rest)
            holding[i] = holding[i] + addition
            rest = rest - addition
    return np.array(holding)


def noise(own_key, dims, scale, limit, pieces=(), kind=jnp.bfloat16):
    array = jax.random.normal(own_key, dims, jnp.float32) * scale
    if len(pieces) > 0:
        array = block_scale(own_key, dims, pieces, -0.22, 0.18) * array
    return jnp.clip(array, min=-limit, max=limit).astype(kind)


def setup_inputs(seed: int = 0) -> dict:
    splits = jax.random.split(jax.random.key(seed), 7)
    initial_state = noise(splits[0], (W,), 1.0, 6.0, (), jnp.float32)
    transition = draw_transition(jax.random.fold_in(splits[6], 71), 0)
    gains = draw_gains(jax.random.fold_in(splits[6], 71), 0)
    tiles = noise(splits[3], (N_GRP, N_SEG * TILE_DEV, W), 4.0, 16.0, ((0, 4), (1, 8)), jnp.float32)
    tile_owner_keys = jax.random.split(jax.random.fold_in(splits[4], 1), N_GRP * (N_SEG * TILE_DEV) // TILE_DEV)
    tile_owner_turns = jax.random.permutation(jax.random.fold_in(splits[4], 3), N_GRP * (N_SEG * TILE_DEV) // TILE_DEV)
    tile_owner = jax.vmap(lambda own, number: routed_block(jax.random.fold_in(splits[4], 2), own, number, TILE_DEV, N_SEG * N_GRP, 1, CAP, 2))(tile_owner_keys, tile_owner_turns).reshape((N_GRP, N_SEG * TILE_DEV, 1))
    tile_step = set_ends(ranked_ids(splits[5], (N_GRP, N_SEG * TILE_DEV), STEP_DEV, 3), jax.random.fold_in(splits[5], 3), 0, STEP_DEV - 1).astype(jnp.int32)
    return {"initial_state": initial_state, "transition": transition, "gains": gains, "tiles": tiles, "tile_owner": tile_owner, "tile_step": tile_step}


def reference(initial_state, transition, gains, tiles, tile_owner, tile_step):
    width = transition.shape[0]
    flat_rows = tiles.reshape(-1, width)
    where_step = (tile_owner.reshape(-1) * STEP_DEV + tile_step.reshape(-1)).astype(jnp.int32)
    obs_sum = jax.ops.segment_sum(flat_rows, where_step, num_segments=STEPS)
    obs_count = jax.ops.segment_sum(jnp.ones(where_step.shape, jnp.float32), where_step, num_segments=STEPS)
    scale = 1.0 / (1.0 + obs_count[:, None] * gains[None, :])

    def advance(state, inputs):
        sums, factor = inputs
        moved = jnp.dot(transition, state, precision=lax.Precision.HIGHEST)
        following = factor * (moved + gains * sums)
        return following, following

    final_state, states = lax.scan(advance, initial_state, (obs_sum, scale))
    return states.reshape(N_GRP, N_SEG * STEP_DEV, width)
```

```python
import functools

import jax
import jax.numpy as jnp
from jax import lax
from jax.experimental import pallas as pl
from jax.experimental.pallas import tpu as pltpu
from jax.sharding import PartitionSpec as P

STEP_DEV = 32
PAIR = 2

F32 = jnp.float32
BF16 = jnp.bfloat16
HIGH = lax.Precision.HIGH
VMEM = pl.BlockSpec(memory_space=pltpu.VMEM)


def split(value):
    upper = value.astype(BF16)
    return upper, (value - upper.astype(F32)).astype(BF16)


def product(upper, lower, right_upper, right_lower):
    dot = functools.partial(jnp.dot, preferred_element_type=F32)
    return dot(upper, right_upper) + dot(lower, right_upper) + dot(upper, right_lower)


def row_times(row, matrix_ref):
    depth, width = matrix_ref.shape
    column = jnp.transpose(jnp.broadcast_to(row, (128, depth)))
    return jnp.concatenate(
        [
            jnp.sum(matrix_ref[:, at : at + 128] * column, axis=0, keepdims=True)
            for at in range(0, width, 128)
        ],
        axis=1,
    )


def map_kernel(moved_ref, scale_ref, half_ref, full_ref, upper_ref, lower_ref):
    share = full_ref.shape[0]
    side = lax.axis_index("seg") % PAIR
    upper, lower = split(moved_ref[...])
    upper_ref[...] = upper
    lower_ref[...] = lower
    rows = pl.ds(pl.multiple_of(side * share, share), share)
    full_ref[...] = moved_ref[rows, :] * scale_ref[pl.ds(0, 1), :]

    def step(at, carry):
        upper, lower = split(full_ref[...])
        joined = product(upper, lower, upper_ref[...], lower_ref[...])
        full_ref[...] = joined * scale_ref[pl.ds(at, 1), :]
        return carry

    lax.fori_loop(1, STEP_DEV, step, 0)
    half_ref[...] = full_ref[...]
    lax.fori_loop(STEP_DEV, PAIR * STEP_DEV, step, 0)


def pair_maps(moved, scale):
    width = moved.shape[0]
    share = width // PAIR
    shape = jax.ShapeDtypeStruct((share, width), F32)
    return pl.pallas_call(
        map_kernel,
        out_shape=(shape, shape),
        in_specs=[VMEM, VMEM],
        out_specs=(VMEM, VMEM),
        scratch_shapes=[pltpu.VMEM((width, width), BF16), pltpu.VMEM((width, width), BF16)],
        compiler_params=pltpu.CompilerParams(vmem_limit_bytes=24 << 20),
        cost_estimate=pl.CostEstimate(
            flops=PAIR * STEP_DEV * 6 * share * width * width,
            bytes_accessed=8 * width * width,
            transcendentals=0,
        ),
    )(moved, scale)


def chain_kernel(
    n_seg,
    n_dev,
    initial_ref,
    moved_ref,
    scale_ref,
    drive_ref,
    half_ref,
    full_ref,
    out_ref,
    into_ref,
    mid_in_ref,
    send_ref,
    mid_send_ref,
    shift_ref,
    state_ref,
    into_sem,
    mid_sem,
    send_sem,
    mid_send_sem,
):
    me = lax.axis_index("grp") * n_seg + lax.axis_index("seg")
    side = me % PAIR
    pair = me // PAIR
    n_pair = n_dev // PAIR
    share = half_ref.shape[0]

    def place(index):
        return {"grp": index // n_seg, "seg": index % n_seg}

    mate = pair * PAIR + 1 - side
    barrier = pltpu.get_barrier_semaphore()
    pl.semaphore_signal(barrier, inc=1, device_id=place(mate))
    for other in range(PAIR):

        @pl.when(pair > 0)
        def _():
            pl.semaphore_signal(barrier, inc=1, device_id=place((pair - 1) * PAIR + other))

        @pl.when(pair < n_pair - 1)
        def _():
            pl.semaphore_signal(barrier, inc=1, device_id=place((pair + 1) * PAIR + other))

    behind = (pair + n_pair - 1) // n_pair
    ahead = 1 - (pair + 1) // n_pair
    pl.semaphore_wait(barrier, 1 + PAIR * (behind + ahead))

    def forced(at, row):
        moved = row_times(row, moved_ref) + drive_ref[pl.ds(at, 1), :]
        return moved * scale_ref[pl.ds(side * STEP_DEV + at, 1), :]

    def unforced(at, row):
        return row_times(row, moved_ref) * scale_ref[pl.ds(at, 1), :]

    shift = lax.fori_loop(0, STEP_DEV, forced, jnp.zeros_like(initial_ref))
    shift_ref[0:1, :] = shift
    shift = lax.fori_loop(STEP_DEV, STEP_DEV + (1 - side) * STEP_DEV, unforced, shift)
    shift_ref[1:2, :] = shift

    @pl.when(pair == 0)
    def _():
        state_ref[...] = initial_ref[...]

    def chain_copy(source, other):
        return pltpu.make_async_remote_copy(
            src_ref=send_ref,
            dst_ref=into_ref.at[source],
            send_sem=send_sem.at[other],
            recv_sem=into_sem.at[source],
            device_id=place((pair + 1) * PAIR + other),
        )

    def mid_copy():
        return pltpu.make_async_remote_copy(
            src_ref=mid_send_ref,
            dst_ref=mid_in_ref,
            send_sem=mid_send_sem,
            recv_sem=mid_sem,
            device_id=place(mate),
        )

    @pl.when(pair > 0)
    def _():
        for source in range(PAIR):
            pltpu.make_async_copy(into_ref.at[source], into_ref.at[source], into_sem.at[source]).wait()
        state_ref[...] = into_ref[0] + into_ref[1]

    mine = state_ref[:, pl.ds(pl.multiple_of(side * share, share), share)]

    @pl.when(pair < n_pair - 1)
    def _():
        send_ref[...] = row_times(mine, full_ref) + shift_ref[1:2, :]
        for source in range(PAIR):

            @pl.when(side == source)
            def _():
                for other in range(PAIR):
                    chain_copy(source, other).start()

    middle = row_times(mine, half_ref)

    @pl.when(side == 0)
    def _():
        mid_send_ref[...] = middle + shift_ref[0:1, :]
        mid_copy().start()
        mid_copy().wait_send()

    @pl.when(side == 1)
    def _():
        pltpu.make_async_copy(mid_in_ref, mid_in_ref, mid_sem).wait()
        state_ref[...] = middle + mid_in_ref[...]

    def advance(at, row):
        row = forced(at, row)
        out_ref[pl.ds(at, 1), :] = row
        return row

    lax.fori_loop(0, STEP_DEV, advance, state_ref[...])

    @pl.when(pair < n_pair - 1)
    def _():
        for other in range(PAIR):
            pltpu.make_async_copy(send_ref, send_ref, send_sem.at[other]).wait()


def chain(n_seg, n_dev, initial, moved, scale, drive, half, full):
    width = moved.shape[0]
    row = pltpu.VMEM((1, width), F32)
    return pl.pallas_call(
        functools.partial(chain_kernel, n_seg, n_dev),
        out_shape=jax.ShapeDtypeStruct((STEP_DEV, width), F32),
        in_specs=[VMEM] * 6,
        out_specs=VMEM,
        scratch_shapes=[
            pltpu.VMEM((PAIR, 1, width), F32),
            row,
            row,
            row,
            pltpu.VMEM((2, width), F32),
            row,
            pltpu.SemaphoreType.DMA((PAIR,)),
            pltpu.SemaphoreType.DMA,
            pltpu.SemaphoreType.DMA((PAIR,)),
            pltpu.SemaphoreType.DMA,
        ],
        compiler_params=pltpu.CompilerParams(
            collective_id=0, has_side_effects=True, vmem_limit_bytes=24 << 20
        ),
    )(initial, moved, scale, drive, half, full)


def on_device(initial_state, transition, gains, tiles, tile_owner, tile_step):
    n_seg = lax.axis_size("seg")
    n_grp = lax.axis_size("grp")
    n_dev = n_seg * n_grp
    me = lax.axis_index("grp") * n_seg + lax.axis_index("seg")
    where_step = tile_owner[0, :, 0] * STEP_DEV + tile_step[0]
    bins = jnp.arange(n_dev * STEP_DEV, dtype=jnp.int32)
    placed = (bins[:, None] == where_step[None, :]).astype(F32)
    counts = lax.psum(jnp.sum(placed, axis=1).reshape(-1, 128), ("grp", "seg")).reshape(-1)
    sums = lax.psum_scatter(
        jnp.dot(placed, tiles[0], precision=HIGH), ("grp", "seg"), scatter_dimension=0, tiled=True
    )
    span = PAIR * STEP_DEV
    pair_counts = lax.dynamic_slice_in_dim(counts, me // PAIR * span, span)
    scale = 1.0 / (1.0 + pair_counts[:, None] * gains[None, :])
    moved = transition.T
    half, full = pair_maps(moved, scale)
    drive = gains[None, :] * sums
    states = chain(n_seg, n_dev, initial_state[None], moved, scale, drive, half, full)
    return states[None]


def solution(mesh):
    in_specs = (P(), P(), P(), P("grp", "seg", None), P("grp", "seg", None), P("grp", "seg"))
    out_specs = P("grp", "seg", None)
    return jax.shard_map(
        on_device, mesh=mesh, in_specs=in_specs, out_specs=out_specs, check_vma=False
    )
```

```python
import functools

import jax
import jax.numpy as jnp
from jax import lax
from jax.experimental import pallas as pl
from jax.experimental.pallas import tpu as pltpu
from jax.sharding import PartitionSpec as P

STEP_DEV = 32
PAIR = 2

F32 = jnp.float32
BF16 = jnp.bfloat16
VMEM = pl.BlockSpec(memory_space=pltpu.VMEM)


def split(value):
    upper = value.astype(BF16)
    return upper, (value - upper.astype(F32)).astype(BF16)


def product(upper, lower, right_upper, right_lower):
    dot = functools.partial(jnp.dot, preferred_element_type=F32)
    return dot(upper, right_upper) + dot(lower, right_upper) + dot(upper, right_lower)


def row_times(row, matrix_ref):
    depth, width = matrix_ref.shape
    column = jnp.transpose(jnp.broadcast_to(row, (128, depth)))
    return jnp.concatenate(
        [
            jnp.sum(matrix_ref[:, at : at + 128] * column, axis=0, keepdims=True)
            for at in range(0, width, 128)
        ],
        axis=1,
    )


def filter_kernel(
    n_seg,
    n_grp,
    initial_ref,
    moved_ref,
    gains_ref,
    counts_ref,
    where_ref,
    tiles_ref,
    out_ref,
    upper_ref,
    lower_ref,
    full_ref,
    half_ref,
    scale_ref,
    drive_ref,
    tile_upper_ref,
    tile_lower_ref,
    counts_in_ref,
    plane_out_ref,
    plane_in_ref,
    plane_sum_ref,
    line_in_ref,
    into_ref,
    mid_in_ref,
    send_ref,
    mid_send_ref,
    shift_ref,
    state_ref,
    counts_sems,
    plane_sems,
    line_sems,
    into_sem,
    mid_sem,
    send_sem,
    mid_send_sem,
):
    n_dev = n_seg * n_grp
    depth = line_in_ref.shape[0] + 1
    inner = n_seg // depth
    n_plane = inner * n_grp
    seg, grp = lax.axis_index("seg"), lax.axis_index("grp")
    me = grp * n_seg + seg
    side = me % PAIR
    pair = me // PAIR
    mate = pair * PAIR + 1 - side
    n_pair = n_dev // PAIR
    share, width = full_ref.shape
    level, spot = seg // inner, grp * inner + seg % inner

    def place(index):
        return {"grp": index // n_seg, "seg": index % n_seg}

    barrier = pltpu.get_barrier_semaphore()

    def greet(at, carry):
        pl.semaphore_signal(barrier, inc=1, device_id=place((me + 1 + at) % n_dev))
        return carry

    lax.fori_loop(0, n_dev - 1, greet, 0)

    row_ids = lax.broadcasted_iota(jnp.int32, (width, width), 0)
    column_ids = lax.broadcasted_iota(jnp.int32, (width, width), 1)
    on_diagonal = row_ids == column_ids
    diagonal = jnp.sum(jnp.where(on_diagonal, moved_ref[...], 0.0), axis=0, keepdims=True)
    upper, lower = split(jnp.where(on_diagonal, 0.0, moved_ref[...]))
    upper_ref[...] = upper
    lower_ref[...] = lower
    upper, lower = split(tiles_ref[...])
    tile_upper_ref[...] = upper
    tile_lower_ref[...] = lower
    pl.semaphore_wait(barrier, n_dev - 1)

    def send_counts(at, carry):
        other = (me + 1 + at) % n_dev
        pltpu.make_async_remote_copy(
            src_ref=counts_ref.at[other // PAIR],
            dst_ref=counts_in_ref.at[at],
            send_sem=counts_sems.at[0],
            recv_sem=counts_sems.at[1],
            device_id=place(other),
        ).start()
        return carry

    lax.fori_loop(0, n_dev - 1, send_counts, 0)

    def binned(other):
        rows = lax.broadcasted_iota(jnp.int32, (depth * STEP_DEV, 1), 0)
        owner = (other // inner) * n_seg + (rows // STEP_DEV) * inner + other % inner
        placed = (owner * STEP_DEV + rows % STEP_DEV == where_ref[...]).astype(F32).astype(BF16)
        dot = functools.partial(jnp.dot, preferred_element_type=F32)
        return dot(placed, tile_upper_ref[...]) + dot(placed, tile_lower_ref[...])

    def send_plane(at, carry):
        other = (spot + 1 + at) % n_plane
        plane_out_ref[at] = binned(other)
        pltpu.make_async_remote_copy(
            src_ref=plane_out_ref.at[at],
            dst_ref=plane_in_ref.at[at],
            send_sem=plane_sems.at[0],
            recv_sem=plane_sems.at[1],
            device_id={"grp": other // inner, "seg": level * inner + other % inner},
        ).start()
        return carry

    lax.fori_loop(0, n_plane - 1, send_plane, 0)
    plane_sum_ref[...] = binned(spot)

    def landed(ref, sem):
        pltpu.make_async_copy(ref, ref, sem).wait()

    landed(counts_in_ref, counts_sems.at[1])
    counts = counts_ref[pair] + jnp.sum(counts_in_ref[...], axis=0)
    column = jnp.transpose(jnp.broadcast_to(counts, (128, 128)))[: PAIR * STEP_DEV]
    for at in range(0, width, 128):
        scale_ref[:, at : at + 128] = 1.0 / (1.0 + column * gains_ref[:, at : at + 128])

    rows = pl.ds(pl.multiple_of(side * share, share), share)
    full_ref[...] = moved_ref[rows, :] * scale_ref[pl.ds(0, 1), :]

    def step(at, carry):
        upper, lower = split(full_ref[...])
        joined = product(upper, lower, upper_ref[...], lower_ref[...])
        full_ref[...] = (joined + full_ref[...] * diagonal) * scale_ref[pl.ds(at, 1), :]
        return carry

    lax.fori_loop(1, STEP_DEV, step, 0)
    half_ref[...] = full_ref[...]
    lax.fori_loop(STEP_DEV, STEP_DEV + STEP_DEV // 4, step, 0)

    landed(plane_in_ref, plane_sems.at[1])
    plane_sum_ref[...] += jnp.sum(plane_in_ref[...], axis=0)

    def level_rows(index):
        return pl.ds(pl.multiple_of(index * STEP_DEV, STEP_DEV), STEP_DEV)

    def send_line(at, carry):
        other = (level + 1 + at) % depth
        pltpu.make_async_remote_copy(
            src_ref=plane_sum_ref.at[level_rows(other)],
            dst_ref=line_in_ref.at[at],
            send_sem=line_sems.at[0],
            recv_sem=line_sems.at[1],
            device_id={"grp": grp, "seg": other * inner + seg % inner},
        ).start()
        return carry

    lax.fori_loop(0, depth - 1, send_line, 0)
    lax.fori_loop(STEP_DEV + STEP_DEV // 4, PAIR * STEP_DEV, step, 0)
    landed(line_in_ref, line_sems.at[1])
    sums = plane_sum_ref[level_rows(level), :] + jnp.sum(line_in_ref[...], axis=0)
    drive_ref[...] = gains_ref[...] * sums

    def forced(at, row):
        moved = row_times(row, moved_ref) + drive_ref[pl.ds(at, 1), :]
        return moved * scale_ref[pl.ds(side * STEP_DEV + at, 1), :]

    def unforced(at, row):
        return row_times(row, moved_ref) * scale_ref[pl.ds(at, 1), :]

    shift = lax.fori_loop(0, STEP_DEV, forced, jnp.zeros_like(initial_ref))
    shift_ref[0:1, :] = shift
    shift = lax.fori_loop(STEP_DEV, STEP_DEV + (1 - side) * STEP_DEV, unforced, shift)
    shift_ref[1:2, :] = shift

    @pl.when(pair == 0)
    def _():
        state_ref[...] = initial_ref[...]

    def chain_copy(source, other):
        return pltpu.make_async_remote_copy(
            src_ref=send_ref,
            dst_ref=into_ref.at[source],
            send_sem=send_sem.at[other],
            recv_sem=into_sem.at[source],
            device_id=place((pair + 1) * PAIR + other),
        )

    def mid_copy():
        return pltpu.make_async_remote_copy(
            src_ref=mid_send_ref,
            dst_ref=mid_in_ref,
            send_sem=mid_send_sem,
            recv_sem=mid_sem,
            device_id=place(mate),
        )

    @pl.when(pair > 0)
    def _():
        for source in range(PAIR):
            pltpu.make_async_copy(into_ref.at[source], into_ref.at[source], into_sem.at[source]).wait()
        state_ref[...] = into_ref[0] + into_ref[1]

    mine = state_ref[:, pl.ds(pl.multiple_of(side * share, share), share)]

    @pl.when(pair < n_pair - 1)
    def _():
        send_ref[...] = row_times(mine, full_ref) + shift_ref[1:2, :]
        for source in range(PAIR):

            @pl.when(side == source)
            def _():
                for other in range(PAIR):
                    chain_copy(source, other).start()

    middle = row_times(mine, half_ref)

    @pl.when(side == 0)
    def _():
        mid_send_ref[...] = middle + shift_ref[0:1, :]
        mid_copy().start()
        mid_copy().wait_send()

    @pl.when(side == 1)
    def _():
        pltpu.make_async_copy(mid_in_ref, mid_in_ref, mid_sem).wait()
        state_ref[...] = middle + mid_in_ref[...]

    def advance(at, row):
        row = forced(at, row)
        out_ref[pl.ds(at, 1), :] = row
        return row

    lax.fori_loop(0, STEP_DEV, advance, state_ref[...])

    @pl.when(pair < n_pair - 1)
    def _():
        for other in range(PAIR):
            pltpu.make_async_copy(send_ref, send_ref, send_sem.at[other]).wait()
    landed(counts_in_ref, counts_sems.at[0])
    landed(plane_out_ref, plane_sems.at[0])
    landed(line_in_ref, line_sems.at[0])


def filtered(n_seg, n_grp, initial, moved, gains, counts, where_step, tiles):
    n_dev = n_seg * n_grp
    depth = 4
    n_plane = n_dev // depth
    tile_count, width = tiles.shape
    share = width // PAIR
    row = pltpu.VMEM((1, width), F32)
    return pl.pallas_call(
        functools.partial(filter_kernel, n_seg, n_grp),
        out_shape=jax.ShapeDtypeStruct((STEP_DEV, width), F32),
        in_specs=[VMEM] * 6,
        out_specs=VMEM,
        scratch_shapes=[
            pltpu.VMEM((width, width), BF16),
            pltpu.VMEM((width, width), BF16),
            pltpu.VMEM((share, width), F32),
            pltpu.VMEM((share, width), F32),
            pltpu.VMEM((PAIR * STEP_DEV, width), F32),
            pltpu.VMEM((STEP_DEV, width), F32),
            pltpu.VMEM((tile_count, width), BF16),
            pltpu.VMEM((tile_count, width), BF16),
            pltpu.VMEM((n_dev - 1, 1, 128), F32),
            pltpu.VMEM((n_plane - 1, depth * STEP_DEV, width), F32),
            pltpu.VMEM((n_plane - 1, depth * STEP_DEV, width), F32),
            pltpu.VMEM((depth * STEP_DEV, width), F32),
            pltpu.VMEM((depth - 1, STEP_DEV, width), F32),
            pltpu.VMEM((PAIR, 1, width), F32),
            row,
            row,
            row,
            pltpu.VMEM((2, width), F32),
            row,
            pltpu.SemaphoreType.DMA((2,)),
            pltpu.SemaphoreType.DMA((2,)),
            pltpu.SemaphoreType.DMA((2,)),
            pltpu.SemaphoreType.DMA((PAIR,)),
            pltpu.SemaphoreType.DMA,
            pltpu.SemaphoreType.DMA((PAIR,)),
            pltpu.SemaphoreType.DMA,
        ],
        compiler_params=pltpu.CompilerParams(
            collective_id=0, has_side_effects=True, vmem_limit_bytes=48 << 20
        ),
    )(initial, moved, gains, counts, where_step, tiles)


def on_device(initial_state, transition, gains, tiles, tile_owner, tile_step):
    n_seg = lax.axis_size("seg")
    n_grp = lax.axis_size("grp")
    where_step = tile_owner[0, :, 0] * STEP_DEV + tile_step[0]
    bins = jnp.arange(n_seg * n_grp * STEP_DEV, dtype=jnp.int32)
    counts = jnp.sum((bins[:, None] == where_step[None, :]).astype(F32), axis=1)
    counts = counts.reshape(-1, 1, PAIR * STEP_DEV)
    counts = jnp.pad(counts, ((0, 0), (0, 0), (0, 128 - PAIR * STEP_DEV)))
    states = filtered(
        n_seg,
        n_grp,
        initial_state[None],
        transition.T,
        gains[None],
        counts,
        where_step[None],
        tiles[0],
    )
    return states[None]


def solution(mesh):
    in_specs = (P(), P(), P(), P("grp", "seg", None), P("grp", "seg", None), P("grp", "seg"))
    out_specs = P("grp", "seg", None)
    return jax.shard_map(
        on_device, mesh=mesh, in_specs=in_specs, out_specs=out_specs, check_vma=False
    )
```

```python
import functools

import jax
import jax.numpy as jnp
from jax import lax
from jax.experimental import pallas as pl
from jax.experimental.pallas import tpu as pltpu
from jax.sharding import PartitionSpec as P

STEP_DEV = 32
PAIR = 2
FIRST = 4

F32 = jnp.float32
BF16 = jnp.bfloat16
VMEM = pl.BlockSpec(memory_space=pltpu.VMEM)


def split(value):
    upper = value.astype(BF16)
    return upper, (value - upper.astype(F32)).astype(BF16)


def product(upper, lower, right_upper, right_lower):
    dot = functools.partial(jnp.dot, preferred_element_type=F32)
    return dot(upper, right_upper) + dot(lower, right_upper) + dot(upper, right_lower)


def row_times(row, matrix_ref):
    depth, width = matrix_ref.shape
    column = jnp.transpose(jnp.broadcast_to(row, (128, depth)))
    return jnp.concatenate(
        [
            jnp.sum(matrix_ref[:, at : at + 128] * column, axis=0, keepdims=True)
            for at in range(0, width, 128)
        ],
        axis=1,
    )


def filter_kernel(
    n_seg,
    n_grp,
    initial_ref,
    transition_ref,
    moved_ref,
    gains_ref,
    counts_ref,
    where_ref,
    tiles_ref,
    out_ref,
    upper_ref,
    lower_ref,
    full_ref,
    half_ref,
    scale_ref,
    column_ref,
    gains_column_ref,
    factors_ref,
    drive_ref,
    drive_columns_ref,
    between_ref,
    tile_upper_ref,
    tile_lower_ref,
    counts_in_ref,
    plane_out_ref,
    plane_in_ref,
    plane_sum_ref,
    line_in_ref,
    into_ref,
    mid_in_ref,
    send_ref,
    mid_send_ref,
    shift_ref,
    state_ref,
    counts_sems,
    plane_sems,
    line_sems,
    into_sem,
    mid_sem,
    send_sem,
    mid_send_sem,
):
    n_dev = n_seg * n_grp
    depth = line_in_ref.shape[0] + 1
    inner = n_seg // depth
    n_plane = inner * n_grp
    seg, grp = lax.axis_index("seg"), lax.axis_index("grp")
    me = grp * n_seg + seg
    side = me % PAIR
    pair = me // PAIR
    mate = pair * PAIR + 1 - side
    n_pair = n_dev // PAIR
    share, width = full_ref.shape
    level, spot = seg // inner, grp * inner + seg % inner

    def place(index):
        return {"grp": index // n_seg, "seg": index % n_seg}

    barrier = pltpu.get_barrier_semaphore()

    def greet(at, carry):
        pl.semaphore_signal(barrier, inc=1, device_id=place((me + 1 + at) % n_dev))
        return carry

    lax.fori_loop(0, n_dev - 1, greet, 0)

    row_ids = lax.broadcasted_iota(jnp.int32, (width, width), 0)
    column_ids = lax.broadcasted_iota(jnp.int32, (width, width), 1)
    on_diagonal = row_ids == column_ids
    diagonal = jnp.sum(jnp.where(on_diagonal, moved_ref[...], 0.0), axis=0, keepdims=True)
    upper, lower = split(jnp.where(on_diagonal, 0.0, moved_ref[...]))
    upper_ref[...] = upper
    lower_ref[...] = lower
    upper, lower = split(tiles_ref[...])
    tile_upper_ref[...] = upper
    tile_lower_ref[...] = lower
    gains_column_ref[...] = jnp.transpose(jnp.broadcast_to(gains_ref[...], (128, width)))
    pl.semaphore_wait(barrier, n_dev - 1)

    def send_counts(at, carry):
        other = (me + 1 + at) % n_dev
        pltpu.make_async_remote_copy(
            src_ref=counts_ref.at[other // PAIR],
            dst_ref=counts_in_ref.at[at],
            send_sem=counts_sems.at[0],
            recv_sem=counts_sems.at[1],
            device_id=place(other),
        ).start()
        return carry

    lax.fori_loop(0, n_dev - 1, send_counts, 0)

    def binned(other):
        rows = lax.broadcasted_iota(jnp.int32, (depth * STEP_DEV, 1), 0)
        owner = (other // inner) * n_seg + (rows // STEP_DEV) * inner + other % inner
        placed = (owner * STEP_DEV + rows % STEP_DEV == where_ref[...]).astype(F32).astype(BF16)
        dot = functools.partial(jnp.dot, preferred_element_type=F32)
        return dot(placed, tile_upper_ref[...]) + dot(placed, tile_lower_ref[...])

    def send_plane(at, carry):
        other = (spot + 1 + at) % n_plane
        plane_out_ref[at] = binned(other)
        pltpu.make_async_remote_copy(
            src_ref=plane_out_ref.at[at],
            dst_ref=plane_in_ref.at[at],
            send_sem=plane_sems.at[0],
            recv_sem=plane_sems.at[1],
            device_id={"grp": other // inner, "seg": level * inner + other % inner},
        ).start()
        return carry

    lax.fori_loop(0, n_plane - 1, send_plane, 0)
    plane_sum_ref[...] = binned(spot)

    def landed(ref, sem):
        pltpu.make_async_copy(ref, ref, sem).wait()

    landed(counts_in_ref, counts_sems.at[1])
    counts = counts_ref[pair] + jnp.sum(counts_in_ref[...], axis=0)
    column = jnp.transpose(jnp.broadcast_to(counts, (128, 128)))[: PAIR * STEP_DEV]
    for at in range(0, width, 128):
        scale_ref[:, at : at + 128] = 1.0 / (1.0 + column * gains_ref[:, at : at + 128])

    half_share = share // 2
    rows = pl.ds(pl.multiple_of(side * share, share), share)
    full_ref[...] = moved_ref[rows, :] * scale_ref[pl.ds(0, 1), :]
    column_ref[...] = column

    def tabulate(entry):
        count = column_ref[pl.ds(2 * entry, 1), :]
        factors_ref[entry] = 1.0 / (1.0 + count * gains_column_ref[...])

    def advance_maps(first, count, entries):
        parts = [full_ref[at : at + half_share, :] for at in (0, half_share)]
        for ahead in range(count):
            factor = scale_ref[pl.ds(first + ahead, 1), :]
            for at in range(2):
                upper, lower = split(parts[at])
                joined = product(upper, lower, upper_ref[...], lower_ref[...])
                parts[at] = (joined + parts[at] * diagonal) * factor
            if ahead < entries:
                tabulate(first + ahead - FIRST)
        for at in range(2):
            full_ref[at * half_share : (at + 1) * half_share, :] = parts[at]

    def early(at, carry):
        advance_maps(FIRST + at * 7, 7, 7)
        return carry

    advance_maps(1, FIRST - 1, 0)
    lax.fori_loop(0, (STEP_DEV - FIRST) // 7, early, 0)
    half_ref[...] = full_ref[...]
    advance_maps(STEP_DEV, 8, 4)

    landed(plane_in_ref, plane_sems.at[1])
    plane_sum_ref[...] += jnp.sum(plane_in_ref[...], axis=0)

    def level_rows(index):
        return pl.ds(pl.multiple_of(index * STEP_DEV, STEP_DEV), STEP_DEV)

    def send_line(at, carry):
        other = (level + 1 + at) % depth
        pltpu.make_async_remote_copy(
            src_ref=plane_sum_ref.at[level_rows(other)],
            dst_ref=line_in_ref.at[at],
            send_sem=line_sems.at[0],
            recv_sem=line_sems.at[1],
            device_id={"grp": grp, "seg": other * inner + seg % inner},
        ).start()
        return carry

    lax.fori_loop(0, depth - 1, send_line, 0)

    def late(at, carry):
        advance_maps(STEP_DEV + 8 + at * 8, 8, 0)
        return carry

    lax.fori_loop(0, STEP_DEV // 8 - 1, late, 0)
    landed(line_in_ref, line_sems.at[1])
    sums = plane_sum_ref[level_rows(level), :] + jnp.sum(line_in_ref[...], axis=0)
    drive_ref[...] = gains_ref[...] * sums
    filler = jnp.zeros((128 - STEP_DEV, width), F32)
    drive_columns_ref[...] = jnp.transpose(jnp.concatenate([drive_ref[...], filler], axis=0))

    lanes = lax.broadcasted_iota(jnp.int32, (width, 128), 1)

    def two_steps(half, at, row, forced):
        position = half * STEP_DEV + at
        moved = transition_ref[:, 0:128] * row[:, 0:128]
        for block in range(128, width, 128):
            moved += transition_ref[:, block : block + 128] * row[:, block : block + 128]
        if forced:
            moved += jnp.where(lanes == at, drive_columns_ref[...], 0.0)
        column = jnp.broadcast_to(jnp.sum(moved, axis=1, keepdims=True), (width, 128))
        column *= factors_ref[position // 2]
        row = jnp.concatenate(
            [
                jnp.sum(moved_ref[:, block : block + 128] * column, axis=0, keepdims=True)
                for block in range(0, width, 128)
            ],
            axis=1,
        )
        if forced:
            row += drive_ref[pl.ds(at + 1, 1), :]
        return row * scale_ref[pl.ds(position + 1, 1), :]

    def forced(at, row):
        return two_steps(side, 2 * at, row, True)

    def unforced(at, row):
        return two_steps(1, 2 * at, row, False)

    shift = lax.fori_loop(0, STEP_DEV // 2, forced, jnp.zeros_like(initial_ref))
    shift_ref[0:1, :] = shift
    shift = lax.fori_loop(0, (1 - side) * (STEP_DEV // 2), unforced, shift)
    shift_ref[1:2, :] = shift

    @pl.when(pair == 0)
    def _():
        state_ref[...] = initial_ref[...]

    def chain_copy(source, other):
        return pltpu.make_async_remote_copy(
            src_ref=send_ref,
            dst_ref=into_ref.at[source],
            send_sem=send_sem.at[other],
            recv_sem=into_sem.at[source],
            device_id=place((pair + 1) * PAIR + other),
        )

    def mid_copy():
        return pltpu.make_async_remote_copy(
            src_ref=mid_send_ref,
            dst_ref=mid_in_ref,
            send_sem=mid_send_sem,
            recv_sem=mid_sem,
            device_id=place(mate),
        )

    @pl.when(pair > 0)
    def _():
        for source in range(PAIR):
            pltpu.make_async_copy(into_ref.at[source], into_ref.at[source], into_sem.at[source]).wait()
        state_ref[...] = into_ref[0] + into_ref[1]

    mine = state_ref[:, pl.ds(pl.multiple_of(side * share, share), share)]

    @pl.when(pair < n_pair - 1)
    def _():
        send_ref[...] = row_times(mine, full_ref) + shift_ref[1:2, :]
        for source in range(PAIR):

            @pl.when(side == source)
            def _():
                for other in range(PAIR):
                    chain_copy(source, other).start()

    middle = row_times(mine, half_ref)

    @pl.when(side == 0)
    def _():
        mid_send_ref[...] = middle + shift_ref[0:1, :]
        mid_copy().start()
        mid_copy().wait_send()

    @pl.when(side == 1)
    def _():
        pltpu.make_async_copy(mid_in_ref, mid_in_ref, mid_sem).wait()
        state_ref[...] = middle + mid_in_ref[...]

    between_ref[...] = jnp.zeros_like(between_ref)
    out_ref[...] = jnp.zeros_like(out_ref)

    def advance(at, row):
        between_ref[pl.ds(2 * at, 1), :] = row
        row = forced(at, row)
        out_ref[pl.ds(2 * at + 1, 1), :] = row
        return row

    lax.fori_loop(0, STEP_DEV // 2, advance, state_ref[...])
    before = between_ref[...]
    upper, lower = split(before)
    moved = product(upper, lower, upper_ref[...], lower_ref[...]) + before * diagonal
    own = pl.ds(pl.multiple_of(side * STEP_DEV, STEP_DEV), STEP_DEV)
    between = (moved + drive_ref[...]) * scale_ref[own, :]
    parity = lax.broadcasted_iota(jnp.int32, (STEP_DEV, width), 0) % 2
    out_ref[...] = jnp.where(parity == 0, between, out_ref[...])

    @pl.when(pair < n_pair - 1)
    def _():
        for other in range(PAIR):
            pltpu.make_async_copy(send_ref, send_ref, send_sem.at[other]).wait()
    landed(counts_in_ref, counts_sems.at[0])
    landed(plane_out_ref, plane_sems.at[0])
    landed(line_in_ref, line_sems.at[0])


def filtered(n_seg, n_grp, initial, transition, moved, gains, counts, where_step, tiles):
    n_dev = n_seg * n_grp
    depth = 4
    n_plane = n_dev // depth
    tile_count, width = tiles.shape
    share = width // PAIR
    row = pltpu.VMEM((1, width), F32)
    return pl.pallas_call(
        functools.partial(filter_kernel, n_seg, n_grp),
        out_shape=jax.ShapeDtypeStruct((STEP_DEV, width), F32),
        in_specs=[VMEM] * 7,
        out_specs=VMEM,
        scratch_shapes=[
            pltpu.VMEM((width, width), BF16),
            pltpu.VMEM((width, width), BF16),
            pltpu.VMEM((share, width), F32),
            pltpu.VMEM((share, width), F32),
            pltpu.VMEM((PAIR * STEP_DEV, width), F32),
            pltpu.VMEM((PAIR * STEP_DEV, 128), F32),
            pltpu.VMEM((width, 128), F32),
            pltpu.VMEM((PAIR * STEP_DEV // 2, width, 128), F32),
            pltpu.VMEM((STEP_DEV, width), F32),
            pltpu.VMEM((width, 128), F32),
            pltpu.VMEM((STEP_DEV, width), F32),
            pltpu.VMEM((tile_count, width), BF16),
            pltpu.VMEM((tile_count, width), BF16),
            pltpu.VMEM((n_dev - 1, 1, 128), F32),
            pltpu.VMEM((n_plane - 1, depth * STEP_DEV, width), F32),
            pltpu.VMEM((n_plane - 1, depth * STEP_DEV, width), F32),
            pltpu.VMEM((depth * STEP_DEV, width), F32),
            pltpu.VMEM((depth - 1, STEP_DEV, width), F32),
            pltpu.VMEM((PAIR, 1, width), F32),
            row,
            row,
            row,
            pltpu.VMEM((2, width), F32),
            row,
            pltpu.SemaphoreType.DMA((2,)),
            pltpu.SemaphoreType.DMA((2,)),
            pltpu.SemaphoreType.DMA((2,)),
            pltpu.SemaphoreType.DMA((PAIR,)),
            pltpu.SemaphoreType.DMA,
            pltpu.SemaphoreType.DMA((PAIR,)),
            pltpu.SemaphoreType.DMA,
        ],
        compiler_params=pltpu.CompilerParams(
            collective_id=0, has_side_effects=True, vmem_limit_bytes=48 << 20
        ),
    )(initial, transition, moved, gains, counts, where_step, tiles)


def on_device(initial_state, transition, gains, tiles, tile_owner, tile_step):
    n_seg = lax.axis_size("seg")
    n_grp = lax.axis_size("grp")
    where_step = tile_owner[0, :, 0] * STEP_DEV + tile_step[0]
    bins = jnp.arange(n_seg * n_grp * STEP_DEV, dtype=jnp.int32)
    counts = jnp.sum((bins[:, None] == where_step[None, :]).astype(F32), axis=1)
    counts = counts.reshape(-1, 1, PAIR * STEP_DEV)
    counts = jnp.pad(counts, ((0, 0), (0, 0), (0, 128 - PAIR * STEP_DEV)))
    states = filtered(
        n_seg,
        n_grp,
        initial_state[None],
        transition,
        transition.T,
        gains[None],
        counts,
        where_step[None],
        tiles[0],
    )
    return states[None]


def solution(mesh):
    in_specs = (P(), P(), P(), P("grp", "seg", None), P("grp", "seg", None), P("grp", "seg"))
    out_specs = P("grp", "seg", None)
    return jax.shard_map(
        on_device, mesh=mesh, in_specs=in_specs, out_specs=out_specs, check_vma=False
    )
```

```python
import functools

import jax
import jax.numpy as jnp
from jax import lax
from jax.experimental import pallas as pl
from jax.experimental.pallas import tpu as pltpu
from jax.sharding import PartitionSpec as P

STEP_DEV = 32
PAIR = 2
FIRST = 4

F32 = jnp.float32
BF16 = jnp.bfloat16
VMEM = pl.BlockSpec(memory_space=pltpu.VMEM)


def split(value):
    upper = value.astype(BF16)
    return upper, (value - upper.astype(F32)).astype(BF16)


def product(upper, lower, right_upper, right_lower):
    dot = functools.partial(jnp.dot, preferred_element_type=F32)
    return dot(upper, right_upper) + dot(lower, right_upper) + dot(upper, right_lower)


def row_times(row, matrix_ref):
    depth, width = matrix_ref.shape
    column = jnp.transpose(jnp.broadcast_to(row, (128, depth)))
    return jnp.concatenate(
        [
            jnp.sum(matrix_ref[:, at : at + 128] * column, axis=0, keepdims=True)
            for at in range(0, width, 128)
        ],
        axis=1,
    )


def filter_kernel(
    n_seg,
    n_grp,
    initial_ref,
    transition_ref,
    moved_ref,
    gains_ref,
    counts_ref,
    where_ref,
    tiles_ref,
    out_ref,
    upper_ref,
    lower_ref,
    full_ref,
    half_ref,
    scale_ref,
    column_ref,
    gains_column_ref,
    factors_ref,
    drive_ref,
    drive_columns_ref,
    between_ref,
    states_ref,
    swap_ref,
    swap_sems,
    tile_upper_ref,
    tile_lower_ref,
    counts_in_ref,
    plane_out_ref,
    plane_in_ref,
    plane_sum_ref,
    line_in_ref,
    into_ref,
    mid_in_ref,
    send_ref,
    mid_send_ref,
    shift_ref,
    state_ref,
    counts_sems,
    plane_sems,
    line_sems,
    into_sem,
    mid_sem,
    send_sem,
    mid_send_sem,
):
    n_dev = n_seg * n_grp
    depth = line_in_ref.shape[0] + 1
    inner = n_seg // depth
    n_plane = inner * n_grp
    seg, grp = lax.axis_index("seg"), lax.axis_index("grp")
    level, spot = seg // inner, grp * inner + seg % inner

    def turned(group, at):
        return at + (depth - 1 - 2 * at) * (group % 2) * (1 - (group + 1) // n_grp)

    def place(index):
        group, at = index // n_seg, index % n_seg
        return {"grp": group, "seg": turned(group, at // inner) * inner + at % inner}

    own_level = turned(grp, level)
    me = grp * n_seg + own_level * inner + seg % inner
    side = me % PAIR
    pair = me // PAIR
    mate = pair * PAIR + 1 - side
    n_pair = n_dev // PAIR
    share, width = full_ref.shape
    barrier = pltpu.get_barrier_semaphore()

    def greet(at, carry):
        pl.semaphore_signal(barrier, inc=1, device_id=place((me + 1 + at) % n_dev))
        return carry

    lax.fori_loop(0, n_dev - 1, greet, 0)

    row_ids = lax.broadcasted_iota(jnp.int32, (width, width), 0)
    column_ids = lax.broadcasted_iota(jnp.int32, (width, width), 1)
    on_diagonal = row_ids == column_ids
    diagonal = jnp.sum(jnp.where(on_diagonal, moved_ref[...], 0.0), axis=0, keepdims=True)
    upper, lower = split(jnp.where(on_diagonal, 0.0, moved_ref[...]))
    upper_ref[...] = upper
    lower_ref[...] = lower
    upper, lower = split(tiles_ref[...])
    tile_upper_ref[...] = upper
    tile_lower_ref[...] = lower
    gains_column_ref[...] = jnp.transpose(jnp.broadcast_to(gains_ref[...], (128, width)))
    pl.semaphore_wait(barrier, n_dev - 1)

    def send_counts(at, carry):
        other = (me + 1 + at) % n_dev
        pltpu.make_async_remote_copy(
            src_ref=counts_ref.at[other // PAIR],
            dst_ref=counts_in_ref.at[at],
            send_sem=counts_sems.at[0],
            recv_sem=counts_sems.at[1],
            device_id=place(other),
        ).start()
        return carry

    lax.fori_loop(0, n_dev - 1, send_counts, 0)

    def binned(other):
        rows = lax.broadcasted_iota(jnp.int32, (depth * STEP_DEV, 1), 0)
        owner = (other // inner) * n_seg + (rows // STEP_DEV) * inner + other % inner
        placed = (owner * STEP_DEV + rows % STEP_DEV == where_ref[...]).astype(F32).astype(BF16)
        dot = functools.partial(jnp.dot, preferred_element_type=F32)
        return dot(placed, tile_upper_ref[...]) + dot(placed, tile_lower_ref[...])

    def send_plane(at, carry):
        other = (spot + 1 + at) % n_plane
        plane_out_ref[at] = binned(other)
        pltpu.make_async_remote_copy(
            src_ref=plane_out_ref.at[at],
            dst_ref=plane_in_ref.at[at],
            send_sem=plane_sems.at[0],
            recv_sem=plane_sems.at[1],
            device_id={"grp": other // inner, "seg": level * inner + other % inner},
        ).start()
        return carry

    lax.fori_loop(0, n_plane - 1, send_plane, 0)
    plane_sum_ref[...] = binned(spot)

    def landed(ref, sem):
        pltpu.make_async_copy(ref, ref, sem).wait()

    landed(counts_in_ref, counts_sems.at[1])
    counts = counts_ref[pair] + jnp.sum(counts_in_ref[...], axis=0)
    column = jnp.transpose(jnp.broadcast_to(counts, (128, 128)))[: PAIR * STEP_DEV]
    for at in range(0, width, 128):
        scale_ref[:, at : at + 128] = 1.0 / (1.0 + column * gains_ref[:, at : at + 128])

    half_share = share // 2
    rows = pl.ds(pl.multiple_of(side * share, share), share)
    full_ref[...] = moved_ref[rows, :] * scale_ref[pl.ds(0, 1), :]
    column_ref[...] = column

    def tabulate(entry):
        count = column_ref[pl.ds(2 * entry, 1), :]
        factors_ref[entry] = 1.0 / (1.0 + count * gains_column_ref[...])

    def advance_maps(first, count, entries):
        parts = [full_ref[at : at + half_share, :] for at in (0, half_share)]
        for ahead in range(count):
            factor = scale_ref[pl.ds(first + ahead, 1), :]
            for at in range(2):
                upper, lower = split(parts[at])
                joined = product(upper, lower, upper_ref[...], lower_ref[...])
                parts[at] = (joined + parts[at] * diagonal) * factor
            if ahead < entries:
                tabulate(first + ahead - FIRST)
        for at in range(2):
            full_ref[at * half_share : (at + 1) * half_share, :] = parts[at]

    def early(at, carry):
        advance_maps(FIRST + at * 7, 7, 7)
        return carry

    advance_maps(1, FIRST - 1, 0)
    lax.fori_loop(0, (STEP_DEV - FIRST) // 7, early, 0)
    half_ref[...] = full_ref[...]
    advance_maps(STEP_DEV, 8, 4)

    landed(plane_in_ref, plane_sems.at[1])
    plane_sum_ref[...] += jnp.sum(plane_in_ref[...], axis=0)

    def level_rows(index):
        return pl.ds(pl.multiple_of(index * STEP_DEV, STEP_DEV), STEP_DEV)

    def send_line(at, carry):
        other = (level + 1 + at) % depth
        pltpu.make_async_remote_copy(
            src_ref=plane_sum_ref.at[level_rows(turned(grp, other))],
            dst_ref=line_in_ref.at[at],
            send_sem=line_sems.at[0],
            recv_sem=line_sems.at[1],
            device_id={"grp": grp, "seg": other * inner + seg % inner},
        ).start()
        return carry

    lax.fori_loop(0, depth - 1, send_line, 0)

    def late(at, carry):
        advance_maps(STEP_DEV + 8 + at * 8, 8, 0)
        return carry

    lax.fori_loop(0, STEP_DEV // 8 - 1, late, 0)
    landed(line_in_ref, line_sems.at[1])
    sums = plane_sum_ref[level_rows(own_level), :] + jnp.sum(line_in_ref[...], axis=0)
    drive_ref[...] = gains_ref[...] * sums
    filler = jnp.zeros((128 - STEP_DEV, width), F32)
    drive_columns_ref[...] = jnp.transpose(jnp.concatenate([drive_ref[...], filler], axis=0))

    lanes = lax.broadcasted_iota(jnp.int32, (width, 128), 1)

    def two_steps(half, at, row, forced):
        position = half * STEP_DEV + at
        moved = transition_ref[:, 0:128] * row[:, 0:128]
        for block in range(128, width, 128):
            moved += transition_ref[:, block : block + 128] * row[:, block : block + 128]
        if forced:
            moved += jnp.where(lanes == at, drive_columns_ref[...], 0.0)
        column = jnp.broadcast_to(jnp.sum(moved, axis=1, keepdims=True), (width, 128))
        column *= factors_ref[position // 2]
        row = jnp.concatenate(
            [
                jnp.sum(moved_ref[:, block : block + 128] * column, axis=0, keepdims=True)
                for block in range(0, width, 128)
            ],
            axis=1,
        )
        if forced:
            row += drive_ref[pl.ds(at + 1, 1), :]
        return row * scale_ref[pl.ds(position + 1, 1), :]

    def forced(at, row):
        return two_steps(side, 2 * at, row, True)

    def unforced(at, row):
        return two_steps(1, 2 * at, row, False)

    shift = lax.fori_loop(0, STEP_DEV // 2, forced, jnp.zeros_like(initial_ref))
    shift_ref[0:1, :] = shift
    shift = lax.fori_loop(0, (1 - side) * (STEP_DEV // 2), unforced, shift)
    shift_ref[1:2, :] = shift

    @pl.when(pair == 0)
    def _():
        state_ref[...] = initial_ref[...]

    def chain_copy(source, other):
        return pltpu.make_async_remote_copy(
            src_ref=send_ref,
            dst_ref=into_ref.at[source],
            send_sem=send_sem.at[other],
            recv_sem=into_sem.at[source],
            device_id=place((pair + 1) * PAIR + other),
        )

    def mid_copy():
        return pltpu.make_async_remote_copy(
            src_ref=mid_send_ref,
            dst_ref=mid_in_ref,
            send_sem=mid_send_sem,
            recv_sem=mid_sem,
            device_id=place(mate),
        )

    @pl.when(pair > 0)
    def _():
        for source in range(PAIR):
            pltpu.make_async_copy(into_ref.at[source], into_ref.at[source], into_sem.at[source]).wait()
        state_ref[...] = into_ref[0] + into_ref[1]

    mine = state_ref[:, pl.ds(pl.multiple_of(side * share, share), share)]

    @pl.when(pair < n_pair - 1)
    def _():
        send_ref[...] = row_times(mine, full_ref) + shift_ref[1:2, :]
        for source in range(PAIR):

            @pl.when(side == source)
            def _():
                for other in range(PAIR):
                    chain_copy(source, other).start()

    middle = row_times(mine, half_ref)

    @pl.when(side == 0)
    def _():
        mid_send_ref[...] = middle + shift_ref[0:1, :]
        mid_copy().start()
        mid_copy().wait_send()

    @pl.when(side == 1)
    def _():
        pltpu.make_async_copy(mid_in_ref, mid_in_ref, mid_sem).wait()
        state_ref[...] = middle + mid_in_ref[...]

    between_ref[...] = jnp.zeros_like(between_ref)
    states_ref[...] = jnp.zeros_like(states_ref)

    def advance(at, row):
        between_ref[pl.ds(2 * at, 1), :] = row
        row = forced(at, row)
        states_ref[pl.ds(2 * at + 1, 1), :] = row
        return row

    lax.fori_loop(0, STEP_DEV // 2, advance, state_ref[...])
    before = between_ref[...]
    upper, lower = split(before)
    moved = product(upper, lower, upper_ref[...], lower_ref[...]) + before * diagonal
    own = pl.ds(pl.multiple_of(side * STEP_DEV, STEP_DEV), STEP_DEV)
    between = (moved + drive_ref[...]) * scale_ref[own, :]
    parity = lax.broadcasted_iota(jnp.int32, (STEP_DEV, width), 0) % 2
    states_ref[...] = jnp.where(parity == 0, between, states_ref[...])
    backwards = (grp % 2) * (1 - (grp + 1) // n_grp)

    @pl.when(backwards == 0)
    def _():
        out_ref[...] = states_ref[...]

    @pl.when(backwards == 1)
    def _():
        swap = pltpu.make_async_remote_copy(
            src_ref=states_ref,
            dst_ref=swap_ref,
            send_sem=swap_sems.at[0],
            recv_sem=swap_sems.at[1],
            device_id={"grp": grp, "seg": (depth - 1 - level) * inner + seg % inner},
        )
        swap.start()
        swap.wait()
        out_ref[...] = swap_ref[...]

    @pl.when(pair < n_pair - 1)
    def _():
        for other in range(PAIR):
            pltpu.make_async_copy(send_ref, send_ref, send_sem.at[other]).wait()
    landed(counts_in_ref, counts_sems.at[0])
    landed(plane_out_ref, plane_sems.at[0])
    landed(line_in_ref, line_sems.at[0])


def filtered(n_seg, n_grp, initial, transition, moved, gains, counts, where_step, tiles):
    n_dev = n_seg * n_grp
    depth = 4
    n_plane = n_dev // depth
    tile_count, width = tiles.shape
    share = width // PAIR
    row = pltpu.VMEM((1, width), F32)
    return pl.pallas_call(
        functools.partial(filter_kernel, n_seg, n_grp),
        out_shape=jax.ShapeDtypeStruct((STEP_DEV, width), F32),
        in_specs=[VMEM] * 7,
        out_specs=VMEM,
        scratch_shapes=[
            pltpu.VMEM((width, width), BF16),
            pltpu.VMEM((width, width), BF16),
            pltpu.VMEM((share, width), F32),
            pltpu.VMEM((share, width), F32),
            pltpu.VMEM((PAIR * STEP_DEV, width), F32),
            pltpu.VMEM((PAIR * STEP_DEV, 128), F32),
            pltpu.VMEM((width, 128), F32),
            pltpu.VMEM((PAIR * STEP_DEV // 2, width, 128), F32),
            pltpu.VMEM((STEP_DEV, width), F32),
            pltpu.VMEM((width, 128), F32),
            pltpu.VMEM((STEP_DEV, width), F32),
            pltpu.VMEM((STEP_DEV, width), F32),
            pltpu.VMEM((STEP_DEV, width), F32),
            pltpu.SemaphoreType.DMA((2,)),
            pltpu.VMEM((tile_count, width), BF16),
            pltpu.VMEM((tile_count, width), BF16),
            pltpu.VMEM((n_dev - 1, 1, 128), F32),
            pltpu.VMEM((n_plane - 1, depth * STEP_DEV, width), F32),
            pltpu.VMEM((n_plane - 1, depth * STEP_DEV, width), F32),
            pltpu.VMEM((depth * STEP_DEV, width), F32),
            pltpu.VMEM((depth - 1, STEP_DEV, width), F32),
            pltpu.VMEM((PAIR, 1, width), F32),
            row,
            row,
            row,
            pltpu.VMEM((2, width), F32),
            row,
            pltpu.SemaphoreType.DMA((2,)),
            pltpu.SemaphoreType.DMA((2,)),
            pltpu.SemaphoreType.DMA((2,)),
            pltpu.SemaphoreType.DMA((PAIR,)),
            pltpu.SemaphoreType.DMA,
            pltpu.SemaphoreType.DMA((PAIR,)),
            pltpu.SemaphoreType.DMA,
        ],
        compiler_params=pltpu.CompilerParams(
            collective_id=0, has_side_effects=True, vmem_limit_bytes=48 << 20
        ),
    )(initial, transition, moved, gains, counts, where_step, tiles)


def on_device(initial_state, transition, gains, tiles, tile_owner, tile_step):
    n_seg = lax.axis_size("seg")
    n_grp = lax.axis_size("grp")
    where_step = tile_owner[0, :, 0] * STEP_DEV + tile_step[0]
    bins = jnp.arange(n_seg * n_grp * STEP_DEV, dtype=jnp.int32)
    counts = jnp.sum((bins[:, None] == where_step[None, :]).astype(F32), axis=1)
    counts = counts.reshape(-1, 1, PAIR * STEP_DEV)
    counts = jnp.pad(counts, ((0, 0), (0, 0), (0, 128 - PAIR * STEP_DEV)))
    states = filtered(
        n_seg,
        n_grp,
        initial_state[None],
        transition,
        transition.T,
        gains[None],
        counts,
        where_step[None],
        tiles[0],
    )
    return states[None]


def solution(mesh):
    in_specs = (P(), P(), P(), P("grp", "seg", None), P("grp", "seg", None), P("grp", "seg"))
    out_specs = P("grp", "seg", None)
    return jax.shard_map(
        on_device, mesh=mesh, in_specs=in_specs, out_specs=out_specs, check_vma=False
    )
```
